32 devices in a mesh: groups: 2 (over y), dec: 16 (over z, x, core).
Axes of the slice: x: 2, y: 2, z: 4, core: 2. Of those that a mesh axis runs over, the one named last changes fastest.
Arguments:
- panels: bfloat16 [512, 64, 512], P(('groups', 'dec')), parts along dimension 0, may hold values from -6 to 6
- tile_panels: int32 [128, 16], P(('groups', 'dec')), parts along dimension 0, may hold values from 0 to 255, as said below
- tile_count: int32 [32], P(('groups', 'dec')), parts along dimension 0, may hold values from 1 to 4, as said below
- conv_weight: bfloat16 [3, 3, 3, 512, 256], replicated, may hold values from -0.0546875 to 0.0546875
- conv_bias: float32 [256], replicated, may hold values from -4 to 4
- norm_gain: float32 [256], replicated, may hold values from 0.1 to 1.9
- norm_shift: float32 [256], replicated, may hold values from -3 to 3
Outputs:
- decoded: bfloat16 [128, 392, 256], P(('groups', 'dec')), parts along dimension 0
The draws below stay inside these ranges and needn't reach their ends.
There are 2 independent parts, one for each index of `groups`. The reference program is written for one: setup_inputs(seed, part) draws one part's arguments, and reference() takes and returns one part's arrays. A program takes and returns all parts, laid end to end along the dimension named above; an argument that names none is the same for every part. Nothing has to cross between parts.
Inputs may be any that keep to these rules, and one draw needn't show every extreme that they name: `tile_panels`: panel p lies on device p // 16. Over all 4 rows of one device, at most 4 entries name panels of any one device, repeats counted; in every draw each device's rows name exactly 4 panels on each of 16 devices. `tile_count`: in every draw some device has 4 live rows.
All inputs are finite; a program needn't handle non-finite values.
Results may differ from the reference program's by a relative error of at most 0.001.
Values may be sent and summed in bfloat16 or wider, within the bound.
No kernel may reach another device: no remote copies, remote signals or barrier semaphores. Data moves between devices by JAX's collectives and lax.ppermute only.
A program may use at most 128 MiB of HBM per device.

```python
import jax
import jax.numpy as jnp
from jax import lax

C_IN = 512
C_OUT = 256
GROUPS = 32
PH = 8
PW = 8
GH = 2
GW = 2
TILE_DEV = 4
PAN_DEV = 16
DECODERS = 16
WT = 4
CELLS = 64
OCELLS = 392
SLOTS = 16
TILES = 64
PANELS = 256
CAP = 4


def permute_row(row_key, values):
    return jax.random.permutation(row_key, values)


def owner_order(row_key):
    return jax.random.permutation(row_key, DECODERS)


def draw_tile_panels(key, part):
    refs_total = TILE_DEV * SLOTS
    order_keys = jax.random.split(jax.random.fold_in(key, 1), DECODERS)
    owners_perm = jax.vmap(owner_order)(order_keys)
    group_of = jnp.arange(refs_total, dtype=jnp.int32) // CAP
    owner_dev = owners_perm[:, group_of]
    local_row = jax.random.randint(jax.random.fold_in(key, 2), (DECODERS, refs_total), 0, PAN_DEV)
    panel_id = owner_dev * PAN_DEV + local_row
    shuffle_keys = jax.random.split(jax.random.fold_in(key, 3), DECODERS)
    shuffled = jax.vmap(permute_row)(shuffle_keys, panel_id)
    return shuffled.reshape(DECODERS * TILE_DEV, SLOTS).astype(jnp.int32)


def draw_tile_count(key, part):
    first_key = jax.random.fold_in(key, 1)
    second_key = jax.random.fold_in(key, 2)
    third_key = jax.random.fold_in(key, 3)
    lottery = jax.random.randint(first_key, (DECODERS,), 0, 10)
    modest = 1 + jax.random.randint(second_key, (DECODERS,), 0, max(1, TILE_DEV // 2))
    counts = jnp.where(lottery < 2, TILE_DEV, modest)
    picked_dev = jax.random.randint(third_key, (), 0, DECODERS)
    return jnp.where(jnp.arange(DECODERS) == picked_dev, TILE_DEV, counts).astype(jnp.int32)


def steps_of(rng, shape, shards, smallest, top_value):
    factor_of, own = 1.0, jax.random.fold_in(rng, 6)
    for dim, parts in shards:
        steps = jnp.exp(jax.random.uniform(jax.random.fold_in(own, dim), (parts,), jnp.float32, smallest / len(shards), top_value / len(shards)))
        factor_of = factor_of * jnp.repeat(steps, shape[dim] // parts).reshape([-1 if axis == dim else 1 for axis in range(len(shape))])
    return factor_of


def scatter_about(key, shape, deviation, limit, shards=(), held_as=jnp.bfloat16):
    drawn = deviation * jax.random.normal(key, shape, jnp.float32)
    if shards:
        drawn = drawn * steps_of(key, shape, shards, -0.22, 0.18)
    return jnp.clip(drawn, -limit, limit).astype(held_as)


def setup_inputs(seed: int = 0, part: int = 0) -> dict:
    key_list = jax.random.split(jax.random.key(seed), 8)
    part_keys = jax.random.split(jax.random.fold_in(key_list[7], part), 8)
    return {
        "panels": scatter_about(part_keys[0], (PANELS, CELLS, C_IN), 1.0, 6.0, ((0, 16),)),
        "tile_panels": draw_tile_panels(jax.random.fold_in(jax.random.fold_in(key_list[7], part), 71), part),
        "tile_count": draw_tile_count(jax.random.fold_in(jax.random.fold_in(key_list[7], part), 71), part),
        "conv_weight": scatter_about(key_list[3], (3, 3, 3, C_IN, C_OUT), (27 * C_IN) ** -0.5, 0.0546875),
        "conv_bias": scatter_about(key_list[4], (C_OUT,), 1.0, 4.0, (), jnp.float32),
        "norm_gain": jnp.clip(1.0 + 0.18 * jax.random.normal(key_list[5], (C_OUT,), jnp.float32), 0.1, 1.9),
        "norm_shift": scatter_about(key_list[6], (C_OUT,), 0.5, 3.0, (), jnp.float32),
    }


epsilon = 1e-06

def arrange_window(panel_rows, frame_count, grid_high, grid_wide, panel_high, panel_wide):
    channels = panel_rows.shape[-1]
    blocks = panel_rows.reshape(frame_count, grid_high, grid_wide, panel_high, panel_wide, channels)
    blocks = blocks.transpose(0, 1, 3, 2, 4, 5)
    return blocks.reshape(frame_count, grid_high * panel_high, grid_wide * panel_wide, channels)

def decode_window(window, kernel, conv_bias, norm_gain, norm_shift, groups):
    out_frames = window.shape[0] - 2
    out_high = window.shape[1] - 2
    out_wide = window.shape[2] - 2
    pieces = []
    for tap_t in range(3):
        for tap_h in range(3):
            for tap_w in range(3):
                pieces.append(window[tap_t:tap_t + out_frames, tap_h:tap_h + out_high, tap_w:tap_w + out_wide, :])
    columns = jnp.concatenate(pieces, axis=-1)
    columns = columns.reshape(out_frames * out_high * out_wide, columns.shape[-1])
    conv_out = jnp.dot(columns, kernel, preferred_element_type=jnp.float32) + conv_bias.astype(jnp.float32)
    cell_count = conv_out.shape[0]
    width_out = conv_out.shape[1]
    grouped = conv_out.reshape(cell_count, groups, width_out // groups)
    center = lax.optimization_barrier(jnp.mean(grouped, axis=(0, 2), keepdims=True))
    shifted = grouped - center
    spread = lax.optimization_barrier(jnp.mean(shifted * shifted, axis=(0, 2), keepdims=True))
    normed = (shifted / jnp.sqrt(spread + epsilon)).reshape(cell_count, width_out)
    scaled = normed * norm_gain.astype(jnp.float32) + norm_shift.astype(jnp.float32)
    return jax.nn.silu(scaled).astype(jnp.bfloat16)

def reference(panels, tile_panels, tile_count, conv_weight, conv_bias, norm_gain, norm_shift):
    kernel = conv_weight.reshape(27 * C_IN, C_OUT)
    tile_index = jnp.arange(TILES, dtype=jnp.int32)
    alive = tile_index % TILE_DEV < tile_count[tile_index // TILE_DEV]

    def single(inputs):
        panel_ids, is_live = inputs

        def active(chosen_ids):
            window = arrange_window(panels[chosen_ids], WT, GH, GW, PH, PW)
            return decode_window(window, kernel, conv_bias, norm_gain, norm_shift, GROUPS)

        def resting(chosen_ids):
            return jnp.zeros((OCELLS, C_OUT), jnp.bfloat16)
        return lax.cond(is_live, active, resting, panel_ids)
    return lax.map(single, (tile_panels, alive))
```

```python
import functools

import jax
import jax.numpy as jnp
import numpy as np
from jax import lax
from jax.experimental import pallas as pl
from jax.experimental.pallas import tpu as pltpu
from jax.sharding import PartitionSpec as P


C_OUT = 256
GROUPS = 32
PH = 8
PW = 8
GH = 2
GW = 2
WT = 4
OF = WT - 2
OH = GH * PH - 2
OW = GW * PW - 2
WIDE = GW * PW
OCELLS = OF * OH * OW
ROWS = OF * OH * WIDE
SPLIT = (256, 256)

epsilon = 1e-06


def requests(tile_panels, live_tiles, per_device, devices, capacity):
    tile_rows, slot_count = tile_panels.shape
    refs = tile_rows * slot_count
    wanted = tile_panels.reshape(refs)
    spot = jnp.arange(refs, dtype=jnp.int32)
    live = spot // slot_count < live_tiles
    owner = jnp.where(live, wanted // per_device, devices)
    local_row = wanted % per_device
    earlier = (owner[None, :] == owner[:, None]) & (spot[None, :] < spot[:, None])
    rank = jnp.sum(earlier.astype(jnp.int32), axis=1)
    where_to = owner * capacity + rank
    places = jnp.arange(devices * capacity, dtype=jnp.int32)
    hit = places[:, None] == where_to[None, :]
    packed = jnp.sum(jnp.where(hit, ((spot + 1) * per_device + local_row)[None, :], 0), axis=1)
    return packed % per_device, packed // per_device - 1


def pick_kernel(half, capacity, which, first, width, place, rows, source, *refs):
    outs, sem = refs[:-1], refs[-1]
    for begin in (True, False):
        for r in range(1, half):
            q = place[1] ^ r
            for k in range(capacity):
                row = rows[(q * 2 + which) * capacity + k]
                copy = pltpu.make_async_copy(
                    source.at[row, :, pl.ds(first, width)], outs[r - 1].at[k], sem.at[r - 1]
                )
                if begin:
                    copy.start()
                else:
                    copy.wait()


def pick(place, rows, source, half, capacity, which, first, width):
    cells = source.shape[1]
    smem = pl.BlockSpec(memory_space=pltpu.SMEM)
    shape = jax.ShapeDtypeStruct((capacity, cells, width), jnp.bfloat16)
    return pl.pallas_call(
        functools.partial(pick_kernel, half, capacity, which, first, width),
        out_shape=[shape] * (half - 1),
        in_specs=[smem, smem, pl.BlockSpec(memory_space=pl.ANY)],
        out_specs=[pl.BlockSpec(memory_space=pltpu.VMEM)] * (half - 1),
        scratch_shapes=[pltpu.SemaphoreType.DMA((half - 1,))],
        compiler_params=pltpu.CompilerParams(vmem_limit_bytes=8 * 2**20),
        cost_estimate=pl.CostEstimate(flops=0, bytes_accessed=4 * 2**20, transcendentals=0),
        name="pick",
    )(place, rows, source)


def conv_tile(window, weights, tile, first, width, between=()):
    sums = [None] * 3
    between = list(between)
    for a in range(3):
        for b in range(3):
            if between:
                between.pop(0)()
            cells = window[tile, a : a + OF, b : b + OH, :, :].reshape(ROWS, width)
            for c in range(3):
                part = jnp.dot(
                    cells,
                    weights[a, b, c, first : first + width],
                    preferred_element_type=jnp.float32,
                )
                sums[c] = part if sums[c] is None else sums[c] + part
    return sums[0] + pltpu.roll(sums[1], ROWS - 1, 0) + pltpu.roll(sums[2], ROWS - 2, 0)


def spread_groups(row):
    lane = lax.broadcasted_iota(jnp.int32, row.shape, 1)
    step = 1
    while step < C_OUT // GROUPS:
        low = (lane // step) % 2 == 0
        row = row + jnp.where(low, pltpu.roll(row, C_OUT - step, 1), pltpu.roll(row, step, 1))
        step *= 2
    return row


def finish_steps(load, take, bias, gain, shift, put):
    count = OCELLS * (C_OUT // GROUPS)
    held = {}

    def total(values):
        column = lax.broadcasted_iota(jnp.int32, (WIDE, C_OUT), 0)
        strip = jnp.where(column < OW, jnp.sum(values, axis=0), 0.0)
        return jnp.sum(strip, axis=0, keepdims=True)

    def strips():
        return load().reshape(OF * OH, WIDE, C_OUT)

    def first():
        held["sum"] = total(strips()) + bias * OCELLS

    def second():
        held["offset"] = bias - spread_groups(held["sum"]) / count

    def third():
        centred = strips() + held["offset"]
        held["square"] = total(centred * centred)

    def fourth():
        var = spread_groups(held["square"]) / count
        held["scale"] = gain / jnp.sqrt(var + epsilon)
        held["base"] = held["offset"] * held["scale"] + shift

    def fifth():
        scaled = load() * held["scale"] + held["base"]
        held["result"] = (scaled / (1.0 + jnp.exp(-scaled))).astype(jnp.bfloat16)

    def sixth():
        picked = jnp.dot(take, held["result"], preferred_element_type=jnp.float32)
        put(picked.astype(jnp.bfloat16))

    return [first, second, third, fourth, fifth, sixth]


def taken_cells():
    cell = np.arange(OCELLS)
    take = np.zeros((OCELLS, ROWS), np.float32)
    take[cell, cell // OW * WIDE + cell % OW] = 1.0
    return jnp.asarray(take, jnp.bfloat16)


def conv_kernel(plan, first, width, is_first, is_last, *refs):
    half, capacity, paired, counts = plan
    live_ref, place, asked, fills, weights = refs[:5]
    refs = refs[5:]
    groups = []
    for count in counts:
        groups.append(refs[:count])
        refs = refs[count:]
    if not is_first:
        partial, refs = refs[0], refs[1:]
    if is_last:
        take, bias, gain, shift = refs[:4]
        refs = refs[4:]
    out, window, result, sem, out_sem = refs[:5]
    rest = refs[5:]
    if not is_first:
        (before, before_sem), rest = rest[:2], rest[2:]
    if is_last:
        sums, blank, blank_sem = rest
    live = live_ref[0]
    slot_count = WT * GH * GW

    def bring(source, tile, slot):
        f, g, h = slot // (GH * GW), slot // GW % GH, slot % GW
        rows = pl.ds(pl.multiple_of(g * PH, PH), PH)
        columns = pl.ds(pl.multiple_of(h * PW, PW), PW)
        return pltpu.make_async_copy(source, window.at[tile, f, rows, columns, :], sem.at[tile])

    def fetch(tile):
        return pltpu.make_async_copy(partial.at[tile], before.at[tile], before_sem.at[tile])

    def store(tile):
        return pltpu.make_async_copy(result.at[tile], out.at[tile], out_sem.at[tile])

    def clear(tile):
        return pltpu.make_async_copy(blank, out.at[tile], blank_sem)

    for side in range(2):
        side_half = place[0] ^ side
        for r in range(half):
            q = place[1] ^ r if paired else r
            for k in range(capacity):
                at = (side_half * half + q) * capacity + k
                spot = fills[at]
                if not paired:
                    source = groups[side][0].at[r * capacity + k]
                elif r == 0:
                    begin = first if side == 0 else 0
                    source = groups[side][0].at[asked[at], :, :, pl.ds(begin, width)]
                else:
                    source = groups[side][r].at[k]

                @pl.when(spot >= 0)
                def _():
                    bring(source, spot // slot_count, spot % slot_count).start()

    if not is_first:

        def prefetch(tile, carry):
            fetch(tile).start()
            return carry

        lax.fori_loop(0, live, prefetch, 0)

    if is_last:
        blank[...] = jnp.zeros((OCELLS, C_OUT), jnp.bfloat16)

        def erase(tile, carry):
            clear(tile).start()
            return carry

        lax.fori_loop(live, result.shape[0], erase, 0)

    def arrive(tile):
        for _ in range(slot_count):
            bring(window.at[tile, 0, pl.ds(0, PH), pl.ds(0, PW), :], tile, 0).wait()
        if not is_first:
            fetch(tile).wait()

    def convolve(tile, between=()):
        conv = conv_tile(window, weights, tile, first, width, between)
        if not is_first:
            conv = conv + before[tile]
        if is_last:
            sums[tile % 2] = conv
        else:
            result[tile] = conv

    def finish(tile):
        if not is_last:
            return []

        def put(values):
            result[tile] = values

        return finish_steps(
            lambda: sums[tile % 2], take[...], bias[...], gain[...], shift[...], put
        )

    arrive(0)
    convolve(0)

    def decode(tile, carry):
        arrive(tile)
        convolve(tile, finish(tile - 1))
        store(tile - 1).start()
        return carry

    lax.fori_loop(1, live, decode, 0)
    for step in finish(live - 1):
        step()
    store(live - 1).start()

    def drain(tile, carry):
        store(tile).wait()
        return carry

    lax.fori_loop(0, live, drain, 0)
    if is_last:

        def drain_blank(tile, carry):
            clear(tile).wait()
            return carry

        lax.fori_loop(live, result.shape[0], drain_blank, 0)


def conv_step(plan, first, width, scalars, weights, arrays, partial, tail, tile_rows):
    smem = pl.BlockSpec(memory_space=pltpu.SMEM)
    hbm = pl.BlockSpec(memory_space=pl.ANY)
    vmem = pl.BlockSpec(memory_space=pltpu.VMEM)
    is_first, is_last = partial is None, tail is not None
    args = [*scalars, weights, *arrays]
    specs = [smem] * len(scalars) + [vmem] + [hbm] * len(arrays)
    sums = (tile_rows, ROWS, C_OUT)
    if is_last:
        result, kind = (tile_rows, OCELLS, C_OUT), jnp.bfloat16
    else:
        result, kind = sums, jnp.float32
    scratch = [
        pltpu.VMEM((tile_rows, WT, GH * PH, WIDE, width), jnp.bfloat16),
        pltpu.VMEM(result, kind),
        pltpu.SemaphoreType.DMA((tile_rows,)),
        pltpu.SemaphoreType.DMA((tile_rows,)),
    ]
    if not is_first:
        args.append(partial)
        specs.append(hbm)
        scratch += [pltpu.VMEM(sums, jnp.float32), pltpu.SemaphoreType.DMA((tile_rows,))]
    if is_last:
        args.extend(tail)
        specs.extend([vmem] * len(tail))
        scratch += [
            pltpu.VMEM((2, ROWS, C_OUT), jnp.float32),
            pltpu.VMEM((OCELLS, C_OUT), jnp.bfloat16),
            pltpu.SemaphoreType.DMA,
        ]
    flops = tile_rows * 2 * ROWS * 27 * width * C_OUT
    return pl.pallas_call(
        functools.partial(conv_kernel, plan, first, width, is_first, is_last),
        out_shape=jax.ShapeDtypeStruct(result, kind),
        in_specs=specs,
        out_specs=hbm,
        scratch_shapes=scratch,
        compiler_params=pltpu.CompilerParams(vmem_limit_bytes=24 * 2**20),
        cost_estimate=pl.CostEstimate(flops=flops, bytes_accessed=8 * 2**20, transcendentals=0),
        name="conv_last" if is_last else "conv_part",
    )(*args)


def decode_tiles(panels, tile_panels, tile_count, conv_weight, conv_bias, norm_gain, norm_shift):
    devices = lax.axis_size("dec")
    tile_rows, slot_count = tile_panels.shape
    per_device, cells, _ = panels.shape
    capacity = max(1, tile_rows * slot_count // devices)
    half = devices // 2
    paired = half <= 8 and half & (half - 1) == 0
    index = lax.axis_index("dec")
    mine, seat = index // half, index % half
    halves = [list(range(half)), list(range(half, devices))]
    swap = [(device, (device + half) % devices) for device in range(devices)]

    asked, fills = requests(tile_panels, tile_count[0], per_device, devices, capacity)
    by_half = asked.reshape(2, half, capacity)
    own_ask = lax.dynamic_index_in_dim(by_half, mine, 0, False)
    far_ask = lax.dynamic_index_in_dim(by_half, 1 - mine, 0, False)
    sent = jnp.stack([own_ask, far_ask], axis=1)
    got = lax.all_to_all(sent, "dec", 0, 0, tiled=True, axis_index_groups=halves)

    firsts = [sum(SPLIT[:n]) for n in range(len(SPLIT))]
    far = []
    source = panels
    for first, width in zip(firsts, SPLIT):
        if far:
            source, far[-1] = lax.optimization_barrier((panels, far[-1]))
        far.append(lax.ppermute(source[:, :, first : first + width], "dec", swap))

    rows = got.reshape(-1)
    place = jnp.stack([mine, seat])

    def exchange(source, which, first, width):
        if not paired:
            picked = source[got[:, which].reshape(-1), :, first : first + width]
            picked = picked.reshape(half, capacity, cells, width)
            landed = lax.all_to_all(picked, "dec", 0, 0, tiled=True, axis_index_groups=halves)
            return [landed.reshape(-1, PH, PW, width)]
        picked = pick(place, rows, source, half, capacity, which, first, width)
        landed = [source.reshape(-1, PH, PW, source.shape[2])]
        for r in range(1, half):
            pairs = [(d, d // half * half + (d % half ^ r)) for d in range(devices)]
            moved = lax.ppermute(picked[r - 1], "dec", pairs)
            landed.append(moved.reshape(capacity, PH, PW, width))
        return landed

    tail = [taken_cells(), *(v.reshape(1, C_OUT) for v in (conv_bias, norm_gain, norm_shift))]
    scalars = (tile_count, place, asked, fills)
    own = []
    for first, width in zip(firsts, SPLIT):
        own.append(exchange(panels, 0, first, width))
    partial = None
    for n, (first, width) in enumerate(zip(firsts, SPLIT)):
        brought = exchange(far[n], 1, 0, width)
        plan = (half, capacity, paired, (len(own[n]), len(brought)))
        partial = conv_step(
            plan, first, width, scalars, conv_weight, [*own[n], *brought], partial,
            tail if n == len(SPLIT) - 1 else None, tile_rows,
        )
    return partial


def solution(mesh):
    in_specs = (
        P(("groups", "dec"), None, None),
        P(("groups", "dec"), None),
        P(("groups", "dec")),
        P(),
        P(),
        P(),
        P(),
    )
    out_specs = P(("groups", "dec"), None, None)
    return jax.shard_map(decode_tiles, mesh=mesh, in_specs=in_specs, out_specs=out_specs, check_vma=False)
```

```python
import functools

import jax
import jax.numpy as jnp
import numpy as np
from jax import lax
from jax.experimental import pallas as pl
from jax.experimental.pallas import tpu as pltpu
from jax.sharding import PartitionSpec as P


C_OUT = 256
GROUPS = 32
PH = 8
PW = 8
GH = 2
GW = 2
WT = 4
OF = WT - 2
OH = GH * PH - 2
OW = GW * PW - 2
WIDE = GW * PW
OCELLS = OF * OH * OW
ROWS = OF * OH * WIDE
SPLIT = (256, 256)

epsilon = 1e-06


def requests(tile_panels, live_tiles, per_device, devices, capacity):
    tile_rows, slot_count = tile_panels.shape
    refs = tile_rows * slot_count
    wanted = tile_panels.reshape(refs)
    spot = jnp.arange(refs, dtype=jnp.int32)
    live = spot // slot_count < live_tiles
    owner = jnp.where(live, wanted // per_device, devices)
    local_row = wanted % per_device
    earlier = (owner[None, :] == owner[:, None]) & (spot[None, :] < spot[:, None])
    rank = jnp.sum(earlier.astype(jnp.int32), axis=1)
    where_to = owner * capacity + rank
    places = jnp.arange(devices * capacity, dtype=jnp.int32)
    hit = places[:, None] == where_to[None, :]
    packed = jnp.sum(jnp.where(hit, ((spot + 1) * per_device + local_row)[None, :], 0), axis=1)
    return packed % per_device, packed // per_device - 1


def pick_kernel(half, capacity, which, first, width, place, rows, source, *refs):
    outs, sem = refs[:-1], refs[-1]
    for begin in (True, False):
        for r in range(half):
            q = place[1] ^ r
            for k in range(capacity):
                row = rows[(q * 2 + which) * capacity + k]
                copy = pltpu.make_async_copy(
                    source.at[row, :, pl.ds(first, width)], outs[r].at[k], sem.at[r]
                )
                if begin:
                    copy.start()
                else:
                    copy.wait()


def pick(place, rows, source, half, capacity, which, first, width):
    cells = source.shape[1]
    smem = pl.BlockSpec(memory_space=pltpu.SMEM)
    shape = jax.ShapeDtypeStruct((capacity, cells, width), jnp.bfloat16)
    return pl.pallas_call(
        functools.partial(pick_kernel, half, capacity, which, first, width),
        out_shape=[shape] * half,
        in_specs=[smem, smem, pl.BlockSpec(memory_space=pl.ANY)],
        out_specs=[pl.BlockSpec(memory_space=pltpu.VMEM)] * half,
        scratch_shapes=[pltpu.SemaphoreType.DMA((half,))],
        compiler_params=pltpu.CompilerParams(vmem_limit_bytes=8 * 2**20),
        cost_estimate=pl.CostEstimate(flops=0, bytes_accessed=0, transcendentals=0),
        name="pick",
    )(place, rows, source)


def conv_tile(window, weights, tile, first, width, between=()):
    sums = [None] * 3
    between = list(between)
    for a in range(3):
        for b in range(3):
            if between:
                between.pop(0)()
            cells = window[tile, a : a + OF, b : b + OH, :, :].reshape(ROWS, width)
            for c in range(3):
                part = jnp.dot(
                    cells,
                    weights[a, b, c, first : first + width],
                    preferred_element_type=jnp.float32,
                )
                sums[c] = part if sums[c] is None else sums[c] + part
    return sums[0] + pltpu.roll(sums[1], ROWS - 1, 0) + pltpu.roll(sums[2], ROWS - 2, 0)


def spread_groups(row):
    lane = lax.broadcasted_iota(jnp.int32, row.shape, 1)
    step = 1
    while step < C_OUT // GROUPS:
        low = (lane // step) % 2 == 0
        row = row + jnp.where(low, pltpu.roll(row, C_OUT - step, 1), pltpu.roll(row, step, 1))
        step *= 2
    return row


def finish_steps(load, take, bias, gain, shift, put):
    count = OCELLS * (C_OUT // GROUPS)
    held = {}

    def total(values):
        column = lax.broadcasted_iota(jnp.int32, (WIDE, C_OUT), 0)
        strip = jnp.where(column < OW, jnp.sum(values, axis=0), 0.0)
        return jnp.sum(strip, axis=0, keepdims=True)

    def strips():
        return load().reshape(OF * OH, WIDE, C_OUT)

    def first():
        held["sum"] = total(strips()) + bias * OCELLS

    def second():
        held["offset"] = bias - spread_groups(held["sum"]) / count

    def third():
        centred = strips() + held["offset"]
        held["square"] = total(centred * centred)

    def fourth():
        var = spread_groups(held["square"]) / count
        held["scale"] = gain / jnp.sqrt(var + epsilon)
        held["base"] = held["offset"] * held["scale"] + shift

    def fifth():
        scaled = load() * held["scale"] + held["base"]
        held["result"] = (scaled / (1.0 + jnp.exp(-scaled))).astype(jnp.bfloat16)

    def sixth():
        picked = jnp.dot(take, held["result"], preferred_element_type=jnp.float32)
        put(picked.astype(jnp.bfloat16))

    return [first, second, third, fourth, fifth, sixth]


def taken_cells():
    cell = np.arange(OCELLS)
    take = np.zeros((OCELLS, ROWS), np.float32)
    take[cell, cell // OW * WIDE + cell % OW] = 1.0
    return jnp.asarray(take, jnp.bfloat16)


def stage_kernel(source, out, sem):
    copy = pltpu.make_async_copy(source, out, sem)
    copy.start()
    copy.wait()


def stage(weights):
    return pl.pallas_call(
        stage_kernel,
        out_shape=jax.ShapeDtypeStruct(weights.shape, weights.dtype),
        in_specs=[pl.BlockSpec(memory_space=pl.ANY)],
        out_specs=pl.BlockSpec(memory_space=pltpu.VMEM),
        scratch_shapes=[pltpu.SemaphoreType.DMA],
        compiler_params=pltpu.CompilerParams(vmem_limit_bytes=12 * 2**20),
        cost_estimate=pl.CostEstimate(flops=0, bytes_accessed=0, transcendentals=0),
        name="stage",
    )(weights)


def conv_kernel(plan, first, width, is_first, is_last, *refs):
    half, capacity, paired, counts = plan
    live_ref, place, fills, weights = refs[:4]
    refs = refs[4:]
    groups = []
    for count in counts:
        groups.append(refs[:count])
        refs = refs[count:]
    if not is_first:
        partial, refs = refs[0], refs[1:]
    if is_last:
        take, bias, gain, shift = refs[:4]
        refs = refs[4:]
    out, window, result, sem, out_sem = refs[:5]
    rest = refs[5:]
    if not is_first:
        (before, before_sem), rest = rest[:2], rest[2:]
    if is_last:
        sums, blank, blank_sem = rest
    live = live_ref[0]
    slot_count = WT * GH * GW

    def bring(source, tile, slot):
        f, g, h = slot // (GH * GW), slot // GW % GH, slot % GW
        rows = pl.ds(pl.multiple_of(g * PH, PH), PH)
        columns = pl.ds(pl.multiple_of(h * PW, PW), PW)
        return pltpu.make_async_copy(source, window.at[tile, f, rows, columns, :], sem.at[tile])

    def fetch(tile):
        return pltpu.make_async_copy(partial.at[tile], before.at[tile], before_sem.at[tile])

    def store(tile):
        return pltpu.make_async_copy(result.at[tile], out.at[tile], out_sem.at[tile])

    def clear(tile):
        return pltpu.make_async_copy(blank, out.at[tile], blank_sem)

    for side in range(2):
        side_half = place[0] ^ side
        for r in range(half):
            q = place[1] ^ r if paired else r
            for k in range(capacity):
                at = (side_half * half + q) * capacity + k
                spot = fills[at]
                if not paired:
                    source = groups[side][0].at[r * capacity + k]
                else:
                    source = groups[side][r].at[k]
                if side == 0:
                    source = source.at[:, :, pl.ds(first, width)]

                @pl.when(spot >= 0)
                def _():
                    bring(source, spot // slot_count, spot % slot_count).start()

    if not is_first:

        def prefetch(tile, carry):
            fetch(tile).start()
            return carry

        lax.fori_loop(0, live, prefetch, 0)

    if is_last:
        blank[...] = jnp.zeros((OCELLS, C_OUT), jnp.bfloat16)

        def erase(tile, carry):
            clear(tile).start()
            return carry

        lax.fori_loop(live, result.shape[0], erase, 0)

    def arrive(tile):
        pltpu.make_async_copy(window.at[tile], window.at[tile], sem.at[tile]).wait()
        if not is_first:
            fetch(tile).wait()

    def convolve(tile, between=()):
        conv = conv_tile(window, weights, tile, first, width, between)
        if not is_first:
            conv = conv + before[tile]
        if is_last:
            sums[tile % 2] = conv
        else:
            result[tile] = conv

    def finish(tile, slot):
        def put(values):
            result[tile] = values

        return finish_steps(lambda: sums[slot], take[...], bias[...], gain[...], shift[...], put)

    def decode(tile, carry):
        arrive(tile)
        if is_last:
            convolve(tile, finish(jnp.maximum(tile - 1, 0), (tile + 1) % 2))

            @pl.when(tile > 0)
            def _():
                store(tile - 1).start()

        else:
            convolve(tile)
            store(tile).start()
        return carry

    lax.fori_loop(0, live, decode, 0)
    if is_last:
        for step in finish(live - 1, (live - 1) % 2):
            step()
        store(live - 1).start()

    def drain(tile, carry):
        store(tile).wait()
        return carry

    lax.fori_loop(0, live, drain, 0)
    if is_last:

        def drain_blank(tile, carry):
            clear(tile).wait()
            return carry

        lax.fori_loop(live, result.shape[0], drain_blank, 0)


def conv_step(plan, first, width, scalars, weights, arrays, partial, tail, tile_rows):
    smem = pl.BlockSpec(memory_space=pltpu.SMEM)
    hbm = pl.BlockSpec(memory_space=pl.ANY)
    vmem = pl.BlockSpec(memory_space=pltpu.VMEM)
    is_first, is_last = partial is None, tail is not None
    args = [*scalars, weights, *arrays]
    specs = [smem] * len(scalars) + [vmem] + [hbm] * len(arrays)
    sums = (tile_rows, ROWS, C_OUT)
    if is_last:
        result, kind = (tile_rows, OCELLS, C_OUT), jnp.bfloat16
    else:
        result, kind = sums, jnp.float32
    scratch = [
        pltpu.VMEM((tile_rows, WT, GH * PH, WIDE, width), jnp.bfloat16),
        pltpu.VMEM(result, kind),
        pltpu.SemaphoreType.DMA((tile_rows,)),
        pltpu.SemaphoreType.DMA((tile_rows,)),
    ]
    if not is_first:
        args.append(partial)
        specs.append(hbm)
        scratch += [pltpu.VMEM(sums, jnp.float32), pltpu.SemaphoreType.DMA((tile_rows,))]
    if is_last:
        args.extend(tail)
        specs.extend([vmem] * len(tail))
        scratch += [
            pltpu.VMEM((2, ROWS, C_OUT), jnp.float32),
            pltpu.VMEM((OCELLS, C_OUT), jnp.bfloat16),
            pltpu.SemaphoreType.DMA,
        ]
    flops = tile_rows * 2 * ROWS * 27 * width * C_OUT
    return pl.pallas_call(
        functools.partial(conv_kernel, plan, first, width, is_first, is_last),
        out_shape=jax.ShapeDtypeStruct(result, kind),
        in_specs=specs,
        out_specs=hbm,
        scratch_shapes=scratch,
        compiler_params=pltpu.CompilerParams(vmem_limit_bytes=24 * 2**20),
        cost_estimate=pl.CostEstimate(flops=flops, bytes_accessed=0, transcendentals=0),
        name="conv_last" if is_last else "conv_part",
    )(*args)


def decode_tiles(panels, tile_panels, tile_count, conv_weight, conv_bias, norm_gain, norm_shift):
    devices = lax.axis_size("dec")
    tile_rows, slot_count = tile_panels.shape
    per_device, cells, channels = panels.shape
    capacity = max(1, tile_rows * slot_count // devices)
    half = devices // 2
    paired = half <= 8 and half & (half - 1) == 0
    index = lax.axis_index("dec")
    mine, seat = index // half, index % half
    halves = [list(range(half)), list(range(half, devices))]
    swap = [(device, (device + half) % devices) for device in range(devices)]

    asked, fills = requests(tile_panels, tile_count[0], per_device, devices, capacity)
    by_half = asked.reshape(2, half, capacity)
    own_ask = lax.dynamic_index_in_dim(by_half, mine, 0, False)
    far_ask = lax.dynamic_index_in_dim(by_half, 1 - mine, 0, False)
    sent = jnp.stack([own_ask, far_ask], axis=1)
    got = lax.all_to_all(sent, "dec", 0, 0, tiled=True, axis_index_groups=halves)

    firsts = [sum(SPLIT[:n]) for n in range(len(SPLIT))]
    far = []
    source = panels
    for first, width in zip(firsts, SPLIT):
        if far:
            source, far[-1] = lax.optimization_barrier((panels, far[-1]))
        far.append(lax.ppermute(source[:, :, first : first + width], "dec", swap))

    rows = got.reshape(-1)
    place = jnp.stack([mine, seat])

    def exchange(source, which, first, width):
        if not paired:
            picked = source[got[:, which].reshape(-1), :, first : first + width]
            picked = picked.reshape(half, capacity, cells, width)
            landed = lax.all_to_all(picked, "dec", 0, 0, tiled=True, axis_index_groups=halves)
            return [landed.reshape(-1, PH, PW, width)]
        picked = pick(place, rows, source, half, capacity, which, first, width)
        landed = [picked[0].reshape(capacity, PH, PW, width)]
        for r in range(1, half):
            pairs = [(d, d // half * half + (d % half ^ r)) for d in range(devices)]
            moved = lax.ppermute(picked[r], "dec", pairs)
            landed.append(moved.reshape(capacity, PH, PW, width))
        return landed

    tail = [taken_cells(), *(v.reshape(1, C_OUT) for v in (conv_bias, norm_gain, norm_shift))]
    scalars = (tile_count, place, fills)
    own = exchange(panels, 0, 0, channels)
    weights = stage(conv_weight)
    partial = None
    for n, (first, width) in enumerate(zip(firsts, SPLIT)):
        brought = exchange(far[n], 1, 0, width)
        plan = (half, capacity, paired, (len(own), len(brought)))
        partial = conv_step(
            plan, first, width, scalars, weights, [*own, *brought], partial,
            tail if n == len(SPLIT) - 1 else None, tile_rows,
        )
    return partial


def solution(mesh):
    in_specs = (
        P(("groups", "dec"), None, None),
        P(("groups", "dec"), None),
        P(("groups", "dec")),
        P(),
        P(),
        P(),
        P(),
    )
    out_specs = P(("groups", "dec"), None, None)
    return jax.shard_map(decode_tiles, mesh=mesh, in_specs=in_specs, out_specs=out_specs, check_vma=False)
```

```python
import functools

import jax
import jax.numpy as jnp
import numpy as np
from jax import lax
from jax.experimental import pallas as pl
from jax.experimental.pallas import tpu as pltpu
from jax.sharding import PartitionSpec as P


C_OUT = 256
GROUPS = 32
PH = 8
PW = 8
GH = 2
GW = 2
WT = 4
OF = WT - 2
OH = GH * PH - 2
OW = GW * PW - 2
WIDE = GW * PW
OCELLS = OF * OH * OW
ROWS = OF * OH * WIDE
SPLIT = (256, 256)

epsilon = 1e-06


def requests(tile_panels, live_tiles, per_device, devices, capacity):
    tile_rows, slot_count = tile_panels.shape
    refs = tile_rows * slot_count
    wanted = tile_panels.reshape(refs)
    spot = jnp.arange(refs, dtype=jnp.int32)
    live = spot // slot_count < live_tiles
    owner = jnp.where(live, wanted // per_device, devices)
    local_row = wanted % per_device
    earlier = (owner[None, :] == owner[:, None]) & (spot[None, :] < spot[:, None])
    rank = jnp.sum(earlier.astype(jnp.int32), axis=1)
    where_to = owner * capacity + rank
    places = jnp.arange(devices * capacity, dtype=jnp.int32)
    hit = places[:, None] == where_to[None, :]
    packed = jnp.sum(jnp.where(hit, ((spot + 1) * per_device + local_row)[None, :], 0), axis=1)
    return packed % per_device, packed // per_device - 1


def pick_kernel(capacity, which, partners, columns, place, rows, *refs):
    count = len(columns)
    sources, outs, sem = refs[:count], refs[count:-1], refs[-1]
    for begin in (True, False):
        for n, r in enumerate(partners):
            q = place[1] ^ r
            for k in range(capacity):
                row = rows[(q * 2 + which) * capacity + k]
                for source, (first, width) in zip(sources, columns):
                    copy = pltpu.make_async_copy(
                        source.at[row], outs[n].at[k, :, pl.ds(first, width)], sem.at[n]
                    )
                    if begin:
                        copy.start()
                    else:
                        copy.wait()


def pick(place, rows, sources, capacity, which, partners):
    cells = sources[0].shape[1]
    widths = [source.shape[2] for source in sources]
    columns = tuple((sum(widths[:n]), widths[n]) for n in range(len(widths)))
    smem = pl.BlockSpec(memory_space=pltpu.SMEM)
    shape = jax.ShapeDtypeStruct((capacity, cells, sum(widths)), jnp.bfloat16)
    return pl.pallas_call(
        functools.partial(pick_kernel, capacity, which, partners, columns),
        out_shape=[shape] * len(partners),
        in_specs=[smem, smem] + [pl.BlockSpec(memory_space=pl.ANY)] * len(sources),
        out_specs=[pl.BlockSpec(memory_space=pltpu.VMEM)] * len(partners),
        scratch_shapes=[pltpu.SemaphoreType.DMA((len(partners),))],
        compiler_params=pltpu.CompilerParams(vmem_limit_bytes=8 * 2**20),
        cost_estimate=pl.CostEstimate(flops=0, bytes_accessed=0, transcendentals=0),
        name="pick",
    )(place, rows, *sources)


def conv_tile(window, weights, tile, first, width, between=()):
    sums = [None] * 3
    between = list(between)
    for a in range(3):
        for b in range(3):
            if between:
                between.pop(0)()
            cells = window[tile, a : a + OF, b : b + OH, :, :].reshape(ROWS, width)
            for c in range(3):
                part = jnp.dot(
                    cells,
                    weights[a, b, c, first : first + width],
                    preferred_element_type=jnp.float32,
                )
                sums[c] = part if sums[c] is None else sums[c] + part
    return sums[0] + pltpu.roll(sums[1], ROWS - 1, 0) + pltpu.roll(sums[2], ROWS - 2, 0)


def spread_groups(row):
    lane = lax.broadcasted_iota(jnp.int32, row.shape, 1)
    step = 1
    while step < C_OUT // GROUPS:
        low = (lane // step) % 2 == 0
        row = row + jnp.where(low, pltpu.roll(row, C_OUT - step, 1), pltpu.roll(row, step, 1))
        step *= 2
    return row


def finish_steps(load, take, bias, gain, shift, put):
    count = OCELLS * (C_OUT // GROUPS)
    held = {}

    def total(values):
        column = lax.broadcasted_iota(jnp.int32, (WIDE, C_OUT), 0)
        strip = jnp.where(column < OW, jnp.sum(values, axis=0), 0.0)
        return jnp.sum(strip, axis=0, keepdims=True)

    def strips():
        return load().reshape(OF * OH, WIDE, C_OUT)

    def first():
        held["sum"] = total(strips()) + bias * OCELLS

    def second():
        held["offset"] = bias - spread_groups(held["sum"]) / count

    def third():
        centred = strips() + held["offset"]
        held["square"] = total(centred * centred)

    def fourth():
        var = spread_groups(held["square"]) / count
        held["scale"] = gain / jnp.sqrt(var + epsilon)
        held["base"] = held["offset"] * held["scale"] + shift

    def fifth():
        scaled = load() * held["scale"] + held["base"]
        held["result"] = (scaled / (1.0 + jnp.exp(-scaled))).astype(jnp.bfloat16)

    def sixth():
        picked = jnp.dot(take, held["result"], preferred_element_type=jnp.float32)
        put(picked.astype(jnp.bfloat16))

    return [first, second, third, fourth, fifth, sixth]


def taken_cells():
    cell = np.arange(OCELLS)
    take = np.zeros((OCELLS, ROWS), np.float32)
    take[cell, cell // OW * WIDE + cell % OW] = 1.0
    return jnp.asarray(take, jnp.bfloat16)


def stage_kernel(source, out, sem):
    copy = pltpu.make_async_copy(source, out, sem)
    copy.start()
    copy.wait()


def stage(weights):
    return pl.pallas_call(
        stage_kernel,
        out_shape=jax.ShapeDtypeStruct(weights.shape, weights.dtype),
        in_specs=[pl.BlockSpec(memory_space=pl.ANY)],
        out_specs=pl.BlockSpec(memory_space=pltpu.VMEM),
        scratch_shapes=[pltpu.SemaphoreType.DMA],
        compiler_params=pltpu.CompilerParams(vmem_limit_bytes=12 * 2**20),
        cost_estimate=pl.CostEstimate(flops=0, bytes_accessed=0, transcendentals=0),
        name="stage",
    )(weights)


def conv_kernel(plan, first, width, is_first, is_last, *refs):
    half, capacity, paired, counts = plan
    live_ref, place, fills, weights = refs[:4]
    refs = refs[4:]
    groups = []
    for count in counts:
        groups.append(refs[:count])
        refs = refs[count:]
    if not is_first:
        partial, refs = refs[0], refs[1:]
    if is_last:
        take, bias, gain, shift = refs[:4]
        refs = refs[4:]
    out, window, result, sem, out_sem = refs[:5]
    rest = refs[5:]
    if not is_first:
        (before, before_sem), rest = rest[:2], rest[2:]
    if is_last:
        sums, blank, blank_sem = rest
    live = live_ref[0]
    slot_count = WT * GH * GW

    def bring(source, tile, slot):
        f, g, h = slot // (GH * GW), slot // GW % GH, slot % GW
        rows = pl.ds(pl.multiple_of(g * PH, PH), PH)
        columns = pl.ds(pl.multiple_of(h * PW, PW), PW)
        return pltpu.make_async_copy(source, window.at[tile, f, rows, columns, :], sem.at[tile])

    def fetch(tile):
        return pltpu.make_async_copy(partial.at[tile], before.at[tile], before_sem.at[tile])

    def store(tile):
        return pltpu.make_async_copy(result.at[tile], out.at[tile], out_sem.at[tile])

    def clear(tile):
        return pltpu.make_async_copy(blank, out.at[tile], blank_sem)

    for side in range(2):
        side_half = place[0] ^ side
        for r in range(half):
            q = place[1] ^ r if paired else r
            for k in range(capacity):
                at = (side_half * half + q) * capacity + k
                spot = fills[at]
                if not paired:
                    source = groups[side][0].at[r * capacity + k]
                else:
                    source = groups[side][r].at[k]
                if side == 0:
                    source = source.at[:, :, pl.ds(first, width)]

                @pl.when(spot >= 0)
                def _():
                    bring(source, spot // slot_count, spot % slot_count).start()

    if not is_first:

        def prefetch(tile, carry):
            fetch(tile).start()
            return carry

        lax.fori_loop(0, live, prefetch, 0)

    if is_last:
        blank[...] = jnp.zeros((OCELLS, C_OUT), jnp.bfloat16)

        def erase(tile, carry):
            clear(tile).start()
            return carry

        lax.fori_loop(live, result.shape[0], erase, 0)

    def arrive(tile):
        pltpu.make_async_copy(window.at[tile], window.at[tile], sem.at[tile]).wait()
        if not is_first:
            fetch(tile).wait()

    def convolve(tile, between=()):
        conv = conv_tile(window, weights, tile, first, width, between)
        if not is_first:
            conv = conv + before[tile]
        if is_last:
            sums[tile % 2] = conv
        else:
            result[tile] = conv

    def finish(tile, slot):
        def put(values):
            result[tile] = values

        return finish_steps(lambda: sums[slot], take[...], bias[...], gain[...], shift[...], put)

    def decode(tile, carry):
        arrive(tile)
        if is_last:
            convolve(tile, finish(jnp.maximum(tile - 1, 0), (tile + 1) % 2))

            @pl.when(tile > 0)
            def _():
                store(tile - 1).start()

        else:
            convolve(tile)
            store(tile).start()
        return carry

    lax.fori_loop(0, live, decode, 0)
    if is_last:
        for step in finish(live - 1, (live - 1) % 2):
            step()
        store(live - 1).start()

    def drain(tile, carry):
        store(tile).wait()
        return carry

    lax.fori_loop(0, live, drain, 0)
    if is_last:

        def drain_blank(tile, carry):
            clear(tile).wait()
            return carry

        lax.fori_loop(live, result.shape[0], drain_blank, 0)


def conv_step(plan, first, width, scalars, weights, arrays, partial, tail, tile_rows):
    smem = pl.BlockSpec(memory_space=pltpu.SMEM)
    hbm = pl.BlockSpec(memory_space=pl.ANY)
    vmem = pl.BlockSpec(memory_space=pltpu.VMEM)
    is_first, is_last = partial is None, tail is not None
    args = [*scalars, weights, *arrays]
    specs = [smem] * len(scalars) + [vmem] + [hbm] * len(arrays)
    sums = (tile_rows, ROWS, C_OUT)
    if is_last:
        result, kind = (tile_rows, OCELLS, C_OUT), jnp.bfloat16
    else:
        result, kind = sums, jnp.float32
    scratch = [
        pltpu.VMEM((tile_rows, WT, GH * PH, WIDE, width), jnp.bfloat16),
        pltpu.VMEM(result, kind),
        pltpu.SemaphoreType.DMA((tile_rows,)),
        pltpu.SemaphoreType.DMA((tile_rows,)),
    ]
    if not is_first:
        args.append(partial)
        specs.append(hbm)
        scratch += [pltpu.VMEM(sums, jnp.float32), pltpu.SemaphoreType.DMA((tile_rows,))]
    if is_last:
        args.extend(tail)
        specs.extend([vmem] * len(tail))
        scratch += [
            pltpu.VMEM((2, ROWS, C_OUT), jnp.float32),
            pltpu.VMEM((OCELLS, C_OUT), jnp.bfloat16),
            pltpu.SemaphoreType.DMA,
        ]
    flops = tile_rows * 2 * ROWS * 27 * width * C_OUT
    return pl.pallas_call(
        functools.partial(conv_kernel, plan, first, width, is_first, is_last),
        out_shape=jax.ShapeDtypeStruct(result, kind),
        in_specs=specs,
        out_specs=hbm,
        scratch_shapes=scratch,
        compiler_params=pltpu.CompilerParams(vmem_limit_bytes=24 * 2**20),
        cost_estimate=pl.CostEstimate(flops=flops, bytes_accessed=0, transcendentals=0),
        name="conv_last" if is_last else "conv_part",
    )(*args)


def partner_sets(half):
    return [tuple(range(half))]


def decode_tiles(panels, tile_panels, tile_count, conv_weight, conv_bias, norm_gain, norm_shift):
    devices = lax.axis_size("dec")
    tile_rows, slot_count = tile_panels.shape
    per_device, cells, _ = panels.shape
    capacity = max(1, tile_rows * slot_count // devices)
    half = devices // 2
    paired = half <= 8 and half & (half - 1) == 0
    index = lax.axis_index("dec")
    mine, seat = index // half, index % half
    halves = [list(range(half)), list(range(half, devices))]
    swap = [(device, (device + half) % devices) for device in range(devices)]

    asked, fills = requests(tile_panels, tile_count[0], per_device, devices, capacity)
    by_half = asked.reshape(2, half, capacity)
    own_ask = lax.dynamic_index_in_dim(by_half, mine, 0, False)
    far_ask = lax.dynamic_index_in_dim(by_half, 1 - mine, 0, False)
    sent = jnp.stack([own_ask, far_ask], axis=1)
    got = lax.all_to_all(sent, "dec", 0, 0, tiled=True, axis_index_groups=halves)

    firsts = [sum(SPLIT[:n]) for n in range(len(SPLIT))]
    parts = [panels[:, :, first : first + width] for first, width in zip(firsts, SPLIT)]
    far = []
    for part in parts:
        if far:
            part, far[-1] = lax.optimization_barrier((part, far[-1]))
        far.append(lax.ppermute(part, "dec", swap))

    rows = got.reshape(-1)
    place = jnp.stack([mine, seat])

    def exchange(sources, which):
        width = sum(source.shape[2] for source in sources)
        if not paired:
            source = sources[0] if len(sources) == 1 else panels
            picked = source[got[:, which].reshape(-1)]
            picked = picked.reshape(half, capacity, cells, width)
            landed = lax.all_to_all(picked, "dec", 0, 0, tiled=True, axis_index_groups=halves)
            return [landed.reshape(-1, PH, PW, width)]
        landed = {}
        for partners in partner_sets(half):
            picked = pick(place, rows, sources, capacity, which, partners)
            for r, array in zip(partners, picked):
                if r > 0:
                    pairs = [(d, d // half * half + (d % half ^ r)) for d in range(devices)]
                    array = lax.ppermute(array, "dec", pairs)
                landed[r] = array.reshape(capacity, PH, PW, width)
        return [landed[r] for r in range(half)]

    tail = [taken_cells(), *(v.reshape(1, C_OUT) for v in (conv_bias, norm_gain, norm_shift))]
    scalars = (tile_count, place, fills)
    own = exchange(parts, 0)
    weights = stage(conv_weight)
    partial = None
    for n, (first, width) in enumerate(zip(firsts, SPLIT)):
        brought = exchange([far[n]], 1)
        plan = (half, capacity, paired, (len(own), len(brought)))
        partial = conv_step(
            plan, first, width, scalars, weights, [*own, *brought], partial,
            tail if n == len(SPLIT) - 1 else None, tile_rows,
        )
    return partial


def solution(mesh):
    in_specs = (
        P(("groups", "dec"), None, None),
        P(("groups", "dec"), None),
        P(("groups", "dec")),
        P(),
        P(),
        P(),
        P(),
    )
    out_specs = P(("groups", "dec"), None, None)
    return jax.shard_map(decode_tiles, mesh=mesh, in_specs=in_specs, out_specs=out_specs, check_vma=False)
```

```python
import functools

import jax
import jax.numpy as jnp
import numpy as np
from jax import lax
from jax.experimental import pallas as pl
from jax.experimental.pallas import tpu as pltpu
from jax.sharding import PartitionSpec as P


C_OUT = 256
GROUPS = 32
PH = 8
PW = 8
GH = 2
GW = 2
WT = 4
OF = WT - 2
OH = GH * PH - 2
OW = GW * PW - 2
WIDE = GW * PW
OCELLS = OF * OH * OW
ROWS = OF * OH * WIDE
SPLIT = (256, 256)

epsilon = 1e-06


def requests(tile_panels, live_tiles, per_device, devices, capacity):
    tile_rows, slot_count = tile_panels.shape
    refs = tile_rows * slot_count
    wanted = tile_panels.reshape(refs)
    spot = jnp.arange(refs, dtype=jnp.int32)
    live = spot // slot_count < live_tiles
    owner = jnp.where(live, wanted // per_device, devices)
    local_row = wanted % per_device
    earlier = (owner[None, :] == owner[:, None]) & (spot[None, :] < spot[:, None])
    rank = jnp.sum(earlier.astype(jnp.int32), axis=1)
    where_to = owner * capacity + rank
    places = jnp.arange(devices * capacity, dtype=jnp.int32)
    hit = places[:, None] == where_to[None, :]
    packed = jnp.sum(jnp.where(hit, ((spot + 1) * per_device + local_row)[None, :], 0), axis=1)
    return packed % per_device, packed // per_device - 1


def pick_kernel(capacity, which, partners, columns, place, rows, *refs):
    count = len(columns)
    sources, outs, sem = refs[:count], refs[count:-1], refs[-1]
    for begin in (True, False):
        for n, r in enumerate(partners):
            q = place[1] ^ r
            for k in range(capacity):
                row = rows[(q * 2 + which) * capacity + k]
                for source, (first, width) in zip(sources, columns):
                    copy = pltpu.make_async_copy(
                        source.at[row], outs[n].at[k, :, pl.ds(first, width)], sem.at[n]
                    )
                    if begin:
                        copy.start()
                    else:
                        copy.wait()


def copy_kernel(capacity, which, partners, place, rows, source, *outs):
    for n, r in enumerate(partners):
        q = place[1] ^ r
        for k in range(capacity):
            outs[n][k] = source[rows[(q * 2 + which) * capacity + k]]


def pick(place, rows, sources, capacity, which, partners):
    cells = sources[0].shape[1]
    widths = [source.shape[2] for source in sources]
    columns = tuple((sum(widths[:n]), widths[n]) for n in range(len(widths)))
    smem = pl.BlockSpec(memory_space=pltpu.SMEM)
    shape = jax.ShapeDtypeStruct((capacity, cells, sum(widths)), jnp.bfloat16)
    if len(sources) == 1:
        vmem = pl.BlockSpec(memory_space=pltpu.VMEM)
        return pl.pallas_call(
            functools.partial(copy_kernel, capacity, which, partners),
            out_shape=[shape] * len(partners),
            in_specs=[smem, smem, vmem],
            out_specs=[vmem] * len(partners),
            compiler_params=pltpu.CompilerParams(vmem_limit_bytes=8 * 2**20),
            cost_estimate=pl.CostEstimate(flops=0, bytes_accessed=0, transcendentals=0),
            name="pick_far",
        )(place, rows, *sources)
    return pl.pallas_call(
        functools.partial(pick_kernel, capacity, which, partners, columns),
        out_shape=[shape] * len(partners),
        in_specs=[smem, smem] + [pl.BlockSpec(memory_space=pl.ANY)] * len(sources),
        out_specs=[pl.BlockSpec(memory_space=pltpu.VMEM)] * len(partners),
        scratch_shapes=[pltpu.SemaphoreType.DMA((len(partners),))],
        compiler_params=pltpu.CompilerParams(vmem_limit_bytes=8 * 2**20),
        cost_estimate=pl.CostEstimate(flops=0, bytes_accessed=0, transcendentals=0),
        name="pick",
    )(place, rows, *sources)


def conv_tile(window, weights, tile, first, width, between=()):
    sums = [None] * 3
    between = list(between)
    for a in range(3):
        for b in range(3):
            if between:
                between.pop(0)()
            cells = window[tile, a : a + OF, b : b + OH, :, :].reshape(ROWS, width)
            for c in range(3):
                part = jnp.dot(
                    cells,
                    weights[a, b, c, first : first + width],
                    preferred_element_type=jnp.float32,
                )
                sums[c] = part if sums[c] is None else sums[c] + part
    return sums[0] + pltpu.roll(sums[1], ROWS - 1, 0) + pltpu.roll(sums[2], ROWS - 2, 0)


def spread_groups(row):
    lane = lax.broadcasted_iota(jnp.int32, row.shape, 1)
    step = 1
    while step < C_OUT // GROUPS:
        low = (lane // step) % 2 == 0
        row = row + jnp.where(low, pltpu.roll(row, C_OUT - step, 1), pltpu.roll(row, step, 1))
        step *= 2
    return row


def finish_steps(load, take, bias, gain, shift, put):
    count = OCELLS * (C_OUT // GROUPS)
    held = {}

    def total(values):
        column = lax.broadcasted_iota(jnp.int32, (WIDE, C_OUT), 0)
        strip = jnp.where(column < OW, jnp.sum(values, axis=0), 0.0)
        return jnp.sum(strip, axis=0, keepdims=True)

    def strips():
        return load().reshape(OF * OH, WIDE, C_OUT)

    def first():
        held["sum"] = total(strips()) + bias * OCELLS

    def second():
        held["offset"] = bias - spread_groups(held["sum"]) / count

    def third():
        centred = strips() + held["offset"]
        held["square"] = total(centred * centred)

    def fourth():
        var = spread_groups(held["square"]) / count
        held["scale"] = gain / jnp.sqrt(var + epsilon)
        held["base"] = held["offset"] * held["scale"] + shift

    def fifth():
        scaled = load() * held["scale"] + held["base"]
        held["result"] = (scaled / (1.0 + jnp.exp(-scaled))).astype(jnp.bfloat16)

    def sixth():
        picked = jnp.dot(take, held["result"], preferred_element_type=jnp.float32)
        put(picked.astype(jnp.bfloat16))

    return [first, second, third, fourth, fifth, sixth]


def taken_cells():
    cell = np.arange(OCELLS)
    take = np.zeros((OCELLS, ROWS), np.float32)
    take[cell, cell // OW * WIDE + cell % OW] = 1.0
    return jnp.asarray(take, jnp.bfloat16)


def stage_kernel(source, out, sem):
    copy = pltpu.make_async_copy(source, out, sem)
    copy.start()
    copy.wait()


def stage(weights):
    return pl.pallas_call(
        stage_kernel,
        out_shape=jax.ShapeDtypeStruct(weights.shape, weights.dtype),
        in_specs=[pl.BlockSpec(memory_space=pl.ANY)],
        out_specs=pl.BlockSpec(memory_space=pltpu.VMEM),
        scratch_shapes=[pltpu.SemaphoreType.DMA],
        compiler_params=pltpu.CompilerParams(vmem_limit_bytes=12 * 2**20),
        cost_estimate=pl.CostEstimate(flops=0, bytes_accessed=0, transcendentals=0),
        name="stage",
    )(weights)


def conv_kernel(plan, first, width, is_first, is_last, *refs):
    half, capacity, paired, counts = plan
    live_ref, place, fills, weights = refs[:4]
    refs = refs[4:]
    groups = []
    for count in counts:
        groups.append(refs[:count])
        refs = refs[count:]
    if not is_first:
        partial, refs = refs[0], refs[1:]
    if is_last:
        take, bias, gain, shift = refs[:4]
        refs = refs[4:]
    out, window, result, sem, out_sem = refs[:5]
    rest = refs[5:]
    if not is_first:
        (before, before_sem), rest = rest[:2], rest[2:]
    if is_last:
        sums, blank, blank_sem = rest
    live = live_ref[0]
    slot_count = WT * GH * GW

    def bring(source, tile, slot):
        f, g, h = slot // (GH * GW), slot // GW % GH, slot % GW
        rows = pl.ds(pl.multiple_of(g * PH, PH), PH)
        columns = pl.ds(pl.multiple_of(h * PW, PW), PW)
        return pltpu.make_async_copy(source, window.at[tile, f, rows, columns, :], sem.at[tile])

    def fetch(tile):
        return pltpu.make_async_copy(partial.at[tile], before.at[tile], before_sem.at[tile])

    def store(tile):
        return pltpu.make_async_copy(result.at[tile], out.at[tile], out_sem.at[tile])

    def clear(tile):
        return pltpu.make_async_copy(blank, out.at[tile], blank_sem)

    for side in range(2):
        side_half = place[0] ^ side
        for r in range(half):
            q = place[1] ^ r if paired else r
            for k in range(capacity):
                at = (side_half * half + q) * capacity + k
                spot = fills[at]
                if not paired:
                    source = groups[side][0].at[r * capacity + k]
                else:
                    source = groups[side][r].at[k]
                if side == 0:
                    source = source.at[:, :, pl.ds(first, width)]

                @pl.when(spot >= 0)
                def _():
                    bring(source, spot // slot_count, spot % slot_count).start()

    if not is_first:

        def prefetch(tile, carry):
            fetch(tile).start()
            return carry

        lax.fori_loop(0, live, prefetch, 0)

    if is_last:
        blank[...] = jnp.zeros((OCELLS, C_OUT), jnp.bfloat16)

        def erase(tile, carry):
            clear(tile).start()
            return carry

        lax.fori_loop(live, result.shape[0], erase, 0)

    def arrive(tile):
        pltpu.make_async_copy(window.at[tile], window.at[tile], sem.at[tile]).wait()
        if not is_first:
            fetch(tile).wait()

    def convolve(tile, between=()):
        conv = conv_tile(window, weights, tile, first, width, between)
        if not is_first:
            conv = conv + before[tile]
        if is_last:
            sums[tile % 2] = conv
        else:
            result[tile] = conv

    def finish(tile, slot):
        def put(values):
            result[tile] = values

        return finish_steps(lambda: sums[slot], take[...], bias[...], gain[...], shift[...], put)

    def decode(tile, carry):
        arrive(tile)
        if is_last:
            convolve(tile, finish(jnp.maximum(tile - 1, 0), (tile + 1) % 2))

            @pl.when(tile > 0)
            def _():
                store(tile - 1).start()

        else:
            convolve(tile)
            store(tile).start()
        return carry

    lax.fori_loop(0, live, decode, 0)
    if is_last:
        for step in finish(live - 1, (live - 1) % 2):
            step()
        store(live - 1).start()

    def drain(tile, carry):
        store(tile).wait()
        return carry

    lax.fori_loop(0, live, drain, 0)
    if is_last:

        def drain_blank(tile, carry):
            clear(tile).wait()
            return carry

        lax.fori_loop(live, result.shape[0], drain_blank, 0)


def conv_step(plan, first, width, scalars, weights, arrays, partial, tail, tile_rows):
    smem = pl.BlockSpec(memory_space=pltpu.SMEM)
    hbm = pl.BlockSpec(memory_space=pl.ANY)
    vmem = pl.BlockSpec(memory_space=pltpu.VMEM)
    is_first, is_last = partial is None, tail is not None
    args = [*scalars, weights, *arrays]
    specs = [smem] * len(scalars) + [vmem] + [hbm] * len(arrays)
    sums = (tile_rows, ROWS, C_OUT)
    if is_last:
        result, kind = (tile_rows, OCELLS, C_OUT), jnp.bfloat16
    else:
        result, kind = sums, jnp.float32
    scratch = [
        pltpu.VMEM((tile_rows, WT, GH * PH, WIDE, width), jnp.bfloat16),
        pltpu.VMEM(result, kind),
        pltpu.SemaphoreType.DMA((tile_rows,)),
        pltpu.SemaphoreType.DMA((tile_rows,)),
    ]
    if not is_first:
        args.append(partial)
        specs.append(hbm)
        scratch += [pltpu.VMEM(sums, jnp.float32), pltpu.SemaphoreType.DMA((tile_rows,))]
    if is_last:
        args.extend(tail)
        specs.extend([vmem] * len(tail))
        scratch += [
            pltpu.VMEM((2, ROWS, C_OUT), jnp.float32),
            pltpu.VMEM((OCELLS, C_OUT), jnp.bfloat16),
            pltpu.SemaphoreType.DMA,
        ]
    flops = tile_rows * 2 * ROWS * 27 * width * C_OUT
    return pl.pallas_call(
        functools.partial(conv_kernel, plan, first, width, is_first, is_last),
        out_shape=jax.ShapeDtypeStruct(result, kind),
        in_specs=specs,
        out_specs=hbm,
        scratch_shapes=scratch,
        compiler_params=pltpu.CompilerParams(vmem_limit_bytes=24 * 2**20),
        cost_estimate=pl.CostEstimate(flops=flops, bytes_accessed=0, transcendentals=0),
        name="conv_last" if is_last else "conv_part",
    )(*args)


def partner_sets(half):
    return [tuple(range(half))]


def decode_tiles(panels, tile_panels, tile_count, conv_weight, conv_bias, norm_gain, norm_shift):
    devices = lax.axis_size("dec")
    tile_rows, slot_count = tile_panels.shape
    per_device, cells, _ = panels.shape
    capacity = max(1, tile_rows * slot_count // devices)
    half = devices // 2
    paired = half <= 8 and half & (half - 1) == 0
    index = lax.axis_index("dec")
    mine, seat = index // half, index % half
    halves = [list(range(half)), list(range(half, devices))]
    swap = [(device, (device + half) % devices) for device in range(devices)]

    asked, fills = requests(tile_panels, tile_count[0], per_device, devices, capacity)
    by_half = asked.reshape(2, half, capacity)
    own_ask = lax.dynamic_index_in_dim(by_half, mine, 0, False)
    far_ask = lax.dynamic_index_in_dim(by_half, 1 - mine, 0, False)
    sent = jnp.stack([own_ask, far_ask], axis=1)
    got = lax.all_to_all(sent, "dec", 0, 0, tiled=True, axis_index_groups=halves)

    firsts = [sum(SPLIT[:n]) for n in range(len(SPLIT))]
    parts = []
    for n, (first, width) in enumerate(zip(firsts, SPLIT)):
        whole = lax.optimization_barrier(panels) if n else panels
        parts.append(whole[:, :, first : first + width])
    far = []
    for part in parts:
        if far:
            part, far[-1] = lax.optimization_barrier((part, far[-1]))
        far.append(lax.ppermute(part, "dec", swap))

    rows = got.reshape(-1)
    place = jnp.stack([mine, seat])

    def exchange(sources, which):
        width = sum(source.shape[2] for source in sources)
        if not paired:
            source = sources[0] if len(sources) == 1 else panels
            picked = source[got[:, which].reshape(-1)]
            picked = picked.reshape(half, capacity, cells, width)
            landed = lax.all_to_all(picked, "dec", 0, 0, tiled=True, axis_index_groups=halves)
            return [landed.reshape(-1, PH, PW, width)]
        landed = {}
        for partners in partner_sets(half):
            picked = pick(place, rows, sources, capacity, which, partners)
            for r, array in zip(partners, picked):
                if r > 0:
                    pairs = [(d, d // half * half + (d % half ^ r)) for d in range(devices)]
                    array = lax.ppermute(array, "dec", pairs)
                landed[r] = array.reshape(capacity, PH, PW, width)
        return [landed[r] for r in range(half)]

    tail = [taken_cells(), *(v.reshape(1, C_OUT) for v in (conv_bias, norm_gain, norm_shift))]
    scalars = (tile_count, place, fills)
    own = exchange(parts, 0)
    weights = stage(conv_weight)
    partial = None
    for n, (first, width) in enumerate(zip(firsts, SPLIT)):
        brought = exchange([far[n]], 1)
        plan = (half, capacity, paired, (len(own), len(brought)))
        partial = conv_step(
            plan, first, width, scalars, weights, [*own, *brought], partial,
            tail if n == len(SPLIT) - 1 else None, tile_rows,
        )
    return partial


def solution(mesh):
    in_specs = (
        P(("groups", "dec"), None, None),
        P(("groups", "dec"), None),
        P(("groups", "dec")),
        P(),
        P(),
        P(),
        P(),
    )
    out_specs = P(("groups", "dec"), None, None)
    return jax.shard_map(decode_tiles, mesh=mesh, in_specs=in_specs, out_specs=out_specs, check_vma=False)
```
